256 devices in a mesh: row: 32 (over y, x, core), col: 8 (over z).
Axes of the slice: x: 4, y: 4, z: 8, core: 2. Of those that a mesh axis runs over, the one named last changes fastest.
Arguments:
- lead_block: float32 [1024, 1024], P('row'), may hold values from -1 to 3, as said below
- panel_block: float32 [16384, 1024], P('row'), may hold values from -1 to 1
- trailing_slab: float32 [16384, 4096], P('row', 'col'), may hold values from -6 to 6
- charge_lead: float32 [1024, 1024], P('row', 'col'), may hold values from -6 to 6
- charge_rest: float32 [16384, 1024], P('row', 'col'), may hold values from -6 to 6
Outputs:
- lead_factor: float32 [1024, 1024], P('row')
- panel_factor: float32 [16384, 1024], P('row')
- slab_updated: float32 [16384, 4096], P('row', 'col')
- solved_lead: float32 [1024, 1024], P('row', 'col')
- charge_updated: float32 [16384, 1024], P('row', 'col')
The draws below stay inside these ranges and needn't reach their ends.
Inputs may be any that keep to these rules, and one draw needn't show every extreme that they name: `lead_block`: symmetric positive definite, smallest eigenvalue above 0.4.
All inputs are finite; a program needn't handle non-finite values.
Results may differ from the reference program's by a relative error of at most 0.00014.
Values sent between devices are 32-bit elements; how exact they have to be, the bound alone decides.
A program may use at most 128 MiB of HBM per device.

```python
import math
import jax
import jax.numpy as jnp
from jax import lax

LEAD = 1024
ROWS = 16384
SLAB_COLS = 4096
NRHS = 1024


def draw_lead_block(key, part):
    first_key = jax.random.fold_in(key, 11)
    second_key = jax.random.fold_in(key, 23)
    normals = jnp.clip(jax.random.normal(first_key, (LEAD, LEAD), jnp.float32), -4.0, 4.0)
    coupled = (normals + normals.T) * (0.35 / math.sqrt(2.0 * LEAD))
    diagonal = jax.random.uniform(second_key, (LEAD,), jnp.float32, 1.2, 2.2)
    identity = jnp.eye(LEAD, dtype=jnp.float32)
    positions = jnp.arange(LEAD, dtype=jnp.float32)
    distance = jnp.abs(positions[:, None] - positions[None, :])
    kernel = 0.6 * jnp.exp(-distance / 8.0)
    return coupled * (1.0 - identity) + identity * diagonal[None, :] + kernel


def block_scale(own_key, dims, shards, smallest, high):
    factor_of, own = 1.0, jax.random.fold_in(own_key, 6)
    for axis_at, shards_of in shards:
        steps = jnp.exp(jax.random.uniform(jax.random.fold_in(own, axis_at), (shards_of,), jnp.float32, smallest / len(shards), high / len(shards)))
        factor_of = factor_of * jnp.repeat(steps, dims[axis_at] // shards_of).reshape([-1 if axis == axis_at else 1 for axis in range(len(dims))])
    return factor_of


def bell_draw(own_key, extent, scale, bound, shards=(), kind=jnp.bfloat16):
    level = block_scale(own_key, extent, shards, -0.22, 0.18) if shards else 1.0
    result = jax.random.normal(own_key, extent, jnp.float32) * scale * level
    return jnp.minimum(jnp.maximum(result, -bound), bound).astype(kind)


def setup_inputs(seed: int = 0) -> dict:
    keys = jax.random.split(jax.random.key(seed), 6)
    lead_block = draw_lead_block(jax.random.fold_in(keys[5], 71), 0)
    panel_block = bell_draw(keys[1], (ROWS, LEAD), 0.125, 1.0, ((0, 32),), jnp.float32)
    trailing_slab = bell_draw(keys[2], (ROWS, SLAB_COLS), 1.0, 6.0, ((0, 32), (1, 8)), jnp.float32)
    charge_lead = bell_draw(keys[3], (LEAD, NRHS), 1.0, 6.0, ((0, 32), (1, 8)), jnp.float32)
    charge_rest = bell_draw(keys[4], (ROWS, NRHS), 1.0, 6.0, ((0, 32), (1, 8)), jnp.float32)
    return dict(lead_block=lead_block, panel_block=panel_block, trailing_slab=trailing_slab, charge_lead=charge_lead, charge_rest=charge_rest)


def factor(matrix):
    half_size = matrix.shape[0] // 2
    first_diag = jnp.linalg.cholesky(matrix[:half_size, :half_size])
    first_below = lax.linalg.triangular_solve(first_diag, matrix[half_size:, :half_size], left_side=False, lower=True, transpose_a=True)
    schur_block = matrix[half_size:, half_size:] - jnp.dot(first_below, first_below.T, precision=lax.Precision.HIGHEST)
    second_diag = jnp.linalg.cholesky(schur_block)
    upper_rows = jnp.concatenate([first_diag, jnp.zeros_like(first_diag)], 1)
    lower_rows = jnp.concatenate([first_below, second_diag], 1)
    return jnp.concatenate([upper_rows, lower_rows], 0)

def reference(lead_block, panel_block, trailing_slab, charge_lead, charge_rest):
    lead_factor = factor(lead_block)
    panel_factor = lax.linalg.triangular_solve(lead_factor, panel_block, left_side=False, lower=True, transpose_a=True)
    slab_rows = panel_factor[:SLAB_COLS]
    slab_updated = trailing_slab - jnp.einsum('ik,jk->ij', panel_factor, slab_rows, precision=lax.Precision.HIGHEST)
    solved_lead = lax.linalg.triangular_solve(lead_factor, charge_lead, left_side=True, lower=True)
    charge_updated = charge_rest - jnp.dot(panel_factor, solved_lead, precision=lax.Precision.HIGHEST)
    return (lead_factor, panel_factor, slab_updated, solved_lead, charge_updated)
```

```python
import collections
import jax
import jax.numpy as jnp
from jax import lax
from jax.experimental import pallas as pl
from jax.experimental.pallas import tpu as pltpu
from jax.sharding import PartitionSpec as P

F32, BF16 = jnp.float32, jnp.bfloat16
B = 128
BLOCKS = 8


def lane(x, i):
    return jnp.broadcast_to(x[:, i:i + 1], (8, B))


def sub(x, j):
    return jnp.broadcast_to(x[j:j + 1, :], (8, B))


def factor(rows, aug, upper, inverse):
    row_of = lax.broadcasted_iota(jnp.int32, (8, B), 0)
    lane_of = lax.broadcasted_iota(jnp.int32, (8, B), 1)
    n = len(rows)
    own = [lane(rows[0], i) for i in range(8)]
    for g in range(n):
        a, b = rows[g], aug[g]
        if g + 1 < n:
            below = [lane(rows[g + 1], 8 * g + i) for i in range(8)]
            after = [lane(rows[g + 1], 8 * g + 8 + i) for i in range(8)]
        dinv = None
        for j in range(8):
            heads = {i: sub(own[i], j) for i in range(j, 8)}
            r = 1.0 / heads[j]
            dinv = r if j == 0 else jnp.where(row_of == j, r, dinv)
            m = jnp.where(row_of > j, own[j] * r, 0.0)
            for i in range(j + 1, 8):
                own[i] = own[i] - m * heads[i]
            if j < 7:
                a = a - m * sub(a, j)
                b = b - m * sub(b, j)
            if g + 1 < n:
                mn = below[j] * r
                for i in range(j + 1, 8):
                    below[i] = below[i] - mn * heads[i]
                for i in range(8):
                    after[i] = after[i] - mn * sub(below[j], i)
            yield
        scale = jnp.sqrt(dinv)
        upper.append(jnp.where(lane_of >= row_of + 8 * g, a * scale, 0.0))
        inverse.append(b * scale)
        if g + 1 < n:
            za, zb = a * dinv, b * dinv
            for j in range(7, 0, -1):
                t = jnp.where(row_of < j, own[j] * dinv, 0.0)
                za = za - t * sub(za, j)
                zb = zb - t * sub(zb, j)
            sa = [sub(za, i) for i in range(8)]
            sb = [sub(zb, i) for i in range(8)]
            for h in range(g + 1, n):
                col = [lane(rows[h], 8 * g + i) for i in range(8)]
                pa = [col[i] * sa[i] for i in range(8)]
                pb = [col[i] * sb[i] for i in range(8)]
                rows[h] = rows[h] - (((pa[0] + pa[1]) + (pa[2] + pa[3])) + ((pa[4] + pa[5]) + (pa[6] + pa[7])))
                aug[h] = aug[h] - (((pb[0] + pb[1]) + (pb[2] + pb[3])) + ((pb[4] + pb[5]) + (pb[6] + pb[7])))
            own = after


def two(x):
    h = x.astype(BF16)
    return h, (x - h.astype(F32)).astype(BF16)


def three(x):
    h = x.astype(BF16)
    r = x - h.astype(F32)
    m = r.astype(BF16)
    return h, m, (r - m.astype(F32)).astype(BF16)


def left6(x):
    h, m, l = three(x)
    return jnp.concatenate([h, h, m, h, m, l], 1)


def right6(x, axis=0):
    h, m, l = three(x)
    return jnp.concatenate([h, m, h, l, m, h], axis)


def left3(x):
    h, l = two(x)
    return jnp.concatenate([h, l, h], 1)


def right3(x, axis=0):
    h, l = two(x)
    return jnp.concatenate([h, h, l], axis)


def mul(x, y):
    return jnp.dot(x, y, preferred_element_type=F32)


def mul_t(x, y):
    return lax.dot_general(x, y, (((1,), (1,)), ((), ())), preferred_element_type=F32)


def at(i):
    return slice(i * B, i * B + B)


class Plan:
    def __init__(self, s, z, c, t, r, rows):
        self.s, self.z, self.c, self.t, self.r = s, z, c, t, r
        self.rows = rows
        self.queue = collections.deque()

    def drain(self, count=None):
        while self.queue and (count is None or count > 0):
            self.queue.popleft()()
            if count is not None:
                count -= 1

    def step(self, k):
        s = self.s
        row_of = lax.broadcasted_iota(jnp.int32, (8, B), 0)
        lane_of = lax.broadcasted_iota(jnp.int32, (8, B), 1)
        rows = [s[k * B + 8 * g:k * B + 8 * g + 8, at(k)] for g in range(16)]
        aug = [jnp.where(lane_of == row_of + 8 * g, 1.0, 0.0).astype(F32) for g in range(16)]
        upper, inverse = [], []
        total = len(self.queue)
        done = 0
        for n, _ in enumerate(factor(rows, aug, upper, inverse)):
            due = min(total, (n + 1) * total // 112)
            self.drain(due - done)
            done = due
        self.drain()
        self.after(k, jnp.concatenate(upper, 0), jnp.concatenate(inverse, 0))

    def after(self, k, upper, w):
        s, z, c, t, r, half = self.s, self.z, self.c, self.t, self.r, self.rows
        add = self.queue.append
        wl = left6(w)
        wt = w.T
        wr = right6(wt)
        wr3 = right3(wt)
        last = BLOCKS - 1
        later = range(k + 1, BLOCKS)
        ql, pr, pr3 = {}, {}, {}

        def panel(j):
            p = mul(wl, right6(s[at(k), at(j)]))
            pr[j] = right6(p)
            pr3[j] = right3(p)

        def column(i):
            q = mul(left6(s[at(i), at(k)]), wr)
            s[at(i), at(k)] = q
            ql[i] = left6(q)

        def trail(i, j):
            s[at(i), at(j)] = s[at(i), at(j)] - mul(ql[i], pr[j])

        def diagonal():
            s[at(k), at(k)] = upper.T

        if k < last:
            panel(k + 1)
            column(k + 1)
            trail(k + 1, k + 1)
            for j in range(k + 2, BLOCKS):
                add(lambda j=j: panel(j))
                add(lambda j=j: column(j))
                if j == k + 2:
                    add(lambda j=j: trail(k + 1, j))
                    add(lambda j=j: trail(j, k + 1))
                    add(lambda j=j: trail(j, j))
            for i in later:
                for j in later:
                    if max(i, j) > k + 2:
                        add(lambda i=i, j=j: trail(i, j))
        add(diagonal)
        xs = {}
        ys = {}

        def solve(m):
            rows = slice(m * 256, m * 256 + 256)
            x = mul(left3(z[rows, at(k)]), wr3)
            z[rows, at(k)] = x
            xs[m] = left3(x)
            if m >= half // 256:
                xs[m, "r"] = right3(x, 1)

        def sweep(m, j, wide):
            rows = slice(m * 256, m * 256 + 256)
            cols = slice(j * B, (j + wide) * B)
            rhs = jnp.concatenate([pr3[j + i] for i in range(wide)], 1)
            z[rows, cols] = z[rows, cols] - mul(xs[m], rhs)

        def right():
            y = mul(left3(w), right3(c[at(k), :]))
            c[at(k), :] = y
            ys[0] = right3(y)

        def right_below(i):
            q = s[at(i), at(k)]
            c[at(i), :] = c[at(i), :] - mul(left3(q), ys[0])

        def slab(m, n):
            rows = slice(m * 256, m * 256 + 256)
            cols = slice(n * 256, n * 256 + 256)
            t[rows, cols] = t[rows, cols] - mul_t(xs[m], xs[n + half // 256, "r"])

        def rest(m):
            rows = slice(m * 256, m * 256 + 256)
            r[rows, :] = r[rows, :] - mul(xs[m], ys[0])

        parts = 2 * half // 256
        for m in range(parts):
            add(lambda m=m: solve(m))
        add(right)
        j = k + 1
        while j < BLOCKS:
            wide = 2 if j + 1 < BLOCKS else 1
            for m in range(parts):
                add(lambda m=m, j=j, wide=wide: sweep(m, j, wide))
            j += wide
        for i in later:
            add(lambda i=i: right_below(i))
        for m in range(half // 256):
            for n in range(t.shape[1] // 256):
                add(lambda m=m, n=n: slab(m, n))
        for m in range(half // 256):
            add(lambda m=m: rest(m))


def whole(s, z, c, t, r, rows):
    plan = Plan(s, z, c, t, r, rows)
    for k in range(BLOCKS):
        plan.step(k)
    plan.drain()


def kernel(lead, panel, far, charge, slab, rest, lead_out, panel_out, slab_out, charge_out, rest_out, s, z, c, sem, out_sem):
    half = panel.shape[0]
    here = [(lead, s), (panel, z.at[0:half]), (far, z.at[half:2 * half]), (charge, c), (slab, slab_out), (rest, rest_out)]
    copies = [pltpu.make_async_copy(a, b, sem.at[i]) for i, (a, b) in enumerate(here)]
    for copy in copies:
        copy.start()
    for copy in copies:
        copy.wait()
    whole(s, z, c, slab_out, rest_out, half)
    count = lead_out.shape[0]
    first = pl.multiple_of(lax.axis_index("row") * count, count)
    column = lax.broadcasted_iota(jnp.int32, lead_out.shape, 1)
    line = lax.broadcasted_iota(jnp.int32, lead_out.shape, 0) + first
    lead_out[...] = jnp.where(column <= line, s[pl.ds(first, count), :], 0.0)
    charge_out[...] = c[pl.ds(first, count), :]
    copy = pltpu.make_async_copy(z.at[0:half], panel_out, out_sem)
    copy.start()
    copy.wait()


def shards(lead_block, panel_block, trailing_slab, charge_lead, charge_rest):
    lead_whole = lax.all_gather(lead_block, "row", axis=0, tiled=True)
    charge_whole = lax.all_gather(charge_lead, "row", axis=0, tiled=True)
    mine = lax.axis_index("row") == lax.axis_index("col")
    far = lax.psum(jnp.where(mine, panel_block, 0.0), "row")
    vmem = pl.BlockSpec(memory_space=pltpu.VMEM)
    hbm = pl.BlockSpec(memory_space=pl.ANY)
    like = lambda a: jax.ShapeDtypeStruct(a.shape, F32)
    lead_mine, lower_panel, slab, solved, rest = pl.pallas_call(
        kernel,
        out_shape=[like(lead_block), like(panel_block), like(trailing_slab), like(charge_lead), like(charge_rest)],
        in_specs=[hbm] * 6,
        out_specs=[vmem, hbm, vmem, vmem, vmem],
        scratch_shapes=[
            pltpu.VMEM(lead_whole.shape, F32),
            pltpu.VMEM((2 * panel_block.shape[0], panel_block.shape[1]), F32),
            pltpu.VMEM(charge_whole.shape, F32),
            pltpu.SemaphoreType.DMA((6,)),
            pltpu.SemaphoreType.DMA,
        ],
        compiler_params=pltpu.CompilerParams(vmem_limit_bytes=56 * 2**20),
    )(lead_whole, panel_block, far, charge_whole, trailing_slab, charge_rest)
    return lead_mine, lower_panel, slab, solved, rest


def solution(mesh):
    placed = (P("row", None), P("row", None), P("row", "col"), P("row", "col"), P("row", "col"))
    return jax.shard_map(shards, mesh=mesh, in_specs=placed, out_specs=placed, check_vma=False)
```

```python
import collections
import jax
import jax.numpy as jnp
from jax import lax
from jax.experimental import pallas as pl
from jax.experimental.pallas import tpu as pltpu
from jax.sharding import PartitionSpec as P

F32, BF16 = jnp.float32, jnp.bfloat16
B = 128
BLOCKS = 8


def lane(x, i):
    return jnp.broadcast_to(x[:, i:i + 1], (8, B))


def sub(x, j):
    return jnp.broadcast_to(x[j:j + 1, :], (8, B))


def factor(rows, aug, upper, inverse):
    row_of = lax.broadcasted_iota(jnp.int32, (8, B), 0)
    lane_of = lax.broadcasted_iota(jnp.int32, (8, B), 1)
    n = len(rows)
    own = [lane(rows[0], i) for i in range(8)]
    for g in range(n):
        a, b = rows[g], aug[g]
        if g + 1 < n:
            below = [lane(rows[g + 1], 8 * g + i) for i in range(8)]
            after = [lane(rows[g + 1], 8 * g + 8 + i) for i in range(8)]
        dinv = None
        for j in range(8):
            heads = {i: sub(own[i], j) for i in range(j, 8)}
            r = 1.0 / heads[j]
            dinv = r if j == 0 else jnp.where(row_of == j, r, dinv)
            m = jnp.where(row_of > j, own[j] * r, 0.0)
            for i in range(j + 1, 8):
                own[i] = own[i] - m * heads[i]
            if j < 7:
                a = a - m * sub(a, j)
                b = b - m * sub(b, j)
            if g + 1 < n:
                mn = below[j] * r
                for i in range(j + 1, 8):
                    below[i] = below[i] - mn * heads[i]
                for i in range(8):
                    after[i] = after[i] - mn * sub(below[j], i)
            yield
        scale = jnp.sqrt(dinv)
        upper.append(jnp.where(lane_of >= row_of + 8 * g, a * scale, 0.0))
        inverse.append(b * scale)
        if g + 1 < n:
            za, zb = a * dinv, b * dinv
            for j in range(7, 0, -1):
                t = jnp.where(row_of < j, own[j] * dinv, 0.0)
                za = za - t * sub(za, j)
                zb = zb - t * sub(zb, j)
            sa = [sub(za, i) for i in range(8)]
            sb = [sub(zb, i) for i in range(8)]
            for h in range(g + 1, n):
                col = [lane(rows[h], 8 * g + i) for i in range(8)]
                pa = [col[i] * sa[i] for i in range(8)]
                pb = [col[i] * sb[i] for i in range(8)]
                rows[h] = rows[h] - (((pa[0] + pa[1]) + (pa[2] + pa[3])) + ((pa[4] + pa[5]) + (pa[6] + pa[7])))
                aug[h] = aug[h] - (((pb[0] + pb[1]) + (pb[2] + pb[3])) + ((pb[4] + pb[5]) + (pb[6] + pb[7])))
            own = after


def two(x):
    h = x.astype(BF16)
    return h, (x - h.astype(F32)).astype(BF16)


def three(x):
    h = x.astype(BF16)
    r = x - h.astype(F32)
    m = r.astype(BF16)
    return h, m, (r - m.astype(F32)).astype(BF16)


def left6(x):
    h, m, l = three(x)
    return jnp.concatenate([h, h, m, h, m, l], 1)


def right6(x, axis=0):
    h, m, l = three(x)
    return jnp.concatenate([h, m, h, l, m, h], axis)


def left3(x):
    h, l = two(x)
    return jnp.concatenate([h, l, h], 1)


def right3(x, axis=0):
    h, l = two(x)
    return jnp.concatenate([h, h, l], axis)


def mul(x, y):
    return jnp.dot(x, y, preferred_element_type=F32)


def mul_t(x, y):
    return lax.dot_general(x, y, (((1,), (1,)), ((), ())), preferred_element_type=F32)


def at(i):
    return slice(i * B, i * B + B)


class Plan:
    def __init__(self, s, z, c, t, r, rows):
        self.s, self.z, self.c, self.t, self.r = s, z, c, t, r
        self.rows = rows
        self.queue = collections.deque()

    def drain(self, count=None):
        while self.queue and (count is None or count > 0):
            self.queue.popleft()()
            if count is not None:
                count -= 1

    def step(self, k):
        s = self.s
        row_of = lax.broadcasted_iota(jnp.int32, (8, B), 0)
        lane_of = lax.broadcasted_iota(jnp.int32, (8, B), 1)
        rows = [s[k * B + 8 * g:k * B + 8 * g + 8, at(k)] for g in range(16)]
        aug = [jnp.where(lane_of == row_of + 8 * g, 1.0, 0.0).astype(F32) for g in range(16)]
        upper, inverse = [], []
        total = len(self.queue)
        done = 0
        for n, _ in enumerate(factor(rows, aug, upper, inverse)):
            due = min(total, (n + 1) * total // 112)
            self.drain(due - done)
            done = due
        self.drain()
        self.after(k, jnp.concatenate(upper, 0), jnp.concatenate(inverse, 0))

    def after(self, k, upper, w):
        s, z, c, t, r, half = self.s, self.z, self.c, self.t, self.r, self.rows
        add = self.queue.append
        wl = left6(w)
        wt = w.T
        wr = right6(wt)
        wr3 = right3(wt)
        last = BLOCKS - 1
        later = range(k + 1, BLOCKS)
        ql, pr, pr3 = {}, {}, {}

        def panel(j):
            p = mul(wl, right6(s[at(k), at(j)]))
            pr[j] = right6(p)
            pr3[j] = right3(p)

        def column(i):
            q = mul(left6(s[at(i), at(k)]), wr)
            s[at(i), at(k)] = q
            ql[i] = left6(q)

        def trail(i, j):
            s[at(i), at(j)] = s[at(i), at(j)] - mul(ql[i], pr[j])

        def diagonal():
            s[at(k), at(k)] = upper.T

        if k < last:
            panel(k + 1)
            column(k + 1)
            trail(k + 1, k + 1)
            for j in range(k + 2, BLOCKS):
                add(lambda j=j: panel(j))
                add(lambda j=j: column(j))
                if j == k + 2:
                    add(lambda j=j: trail(k + 1, j))
                    add(lambda j=j: trail(j, k + 1))
                    add(lambda j=j: trail(j, j))
            for i in later:
                for j in later:
                    if max(i, j) > k + 2:
                        add(lambda i=i, j=j: trail(i, j))
        add(diagonal)
        xs = {}
        ys = {}

        def solve(m):
            rows = slice(m * 256, m * 256 + 256)
            x = mul(left3(z[rows, at(k)]), wr3)
            z[rows, at(k)] = x
            xs[m] = left3(x)
            if m >= half // 256:
                xs[m, "r"] = right3(x, 1)

        def sweep(m, j, wide):
            rows = slice(m * 256, m * 256 + 256)
            cols = slice(j * B, (j + wide) * B)
            rhs = jnp.concatenate([pr3[j + i] for i in range(wide)], 1)
            z[rows, cols] = z[rows, cols] - mul(xs[m], rhs)

        def right():
            y = mul(left3(w), right3(c[at(k), :]))
            c[at(k), :] = y
            ys[0] = right3(y)

        def right_below(i):
            q = s[at(i), at(k)]
            c[at(i), :] = c[at(i), :] - mul(left3(q), ys[0])

        def slab(m, n):
            rows = slice(m * 256, m * 256 + 256)
            cols = slice(n * 256, n * 256 + 256)
            t[rows, cols] = t[rows, cols] - mul_t(xs[m], xs[n + half // 256, "r"])

        def rest(m):
            rows = slice(m * 256, m * 256 + 256)
            r[rows, :] = r[rows, :] - mul(xs[m], ys[0])

        parts = 2 * half // 256
        for m in range(parts):
            add(lambda m=m: solve(m))
        add(right)
        j = k + 1
        while j < BLOCKS:
            wide = 2 if j + 1 < BLOCKS else 1
            for m in range(parts):
                add(lambda m=m, j=j, wide=wide: sweep(m, j, wide))
            j += wide
        for i in later:
            add(lambda i=i: right_below(i))
        for m in range(half // 256):
            for n in range(t.shape[1] // 256):
                add(lambda m=m, n=n: slab(m, n))
        for m in range(half // 256):
            add(lambda m=m: rest(m))


def whole(s, z, c, t, r, rows):
    plan = Plan(s, z, c, t, r, rows)
    for k in range(BLOCKS):
        plan.step(k)
    plan.drain()


def kernel(lead, panel, far, charge, slab, rest, lead_out, panel_out, slab_out, charge_out, rest_out, s, z, c, sem, out_sem):
    half = panel.shape[0]
    here = [(lead, s), (panel, z.at[0:half]), (far, z.at[half:2 * half]), (charge, c), (slab, slab_out), (rest, rest_out)]
    copies = [pltpu.make_async_copy(a, b, sem.at[i]) for i, (a, b) in enumerate(here)]
    for copy in copies:
        copy.start()
    for copy in copies:
        copy.wait()
    whole(s, z, c, slab_out, rest_out, half)
    count = lead_out.shape[0]
    first = pl.multiple_of(lax.axis_index("row") * count, count)
    column = lax.broadcasted_iota(jnp.int32, lead_out.shape, 1)
    line = lax.broadcasted_iota(jnp.int32, lead_out.shape, 0) + first
    lead_out[...] = jnp.where(column <= line, s[pl.ds(first, count), :], 0.0)
    charge_out[...] = c[pl.ds(first, count), :]
    copy = pltpu.make_async_copy(z.at[0:half], panel_out, out_sem)
    copy.start()
    copy.wait()


MESH = pl.DeviceIdType.MESH


def gather(lead, panel, charge, lead_all, far_all, charge_all, send_sem, recv_sem, far_send, far_recv, spread_sem, local_sem):
    row, col = lax.axis_index("row"), lax.axis_index("col")
    core, chip = row % 2, row // 2
    x, y = chip % 4, chip // 4
    u = x * (1 - core) + y * core
    v = y * (1 - core) + x * core

    def place(a, b, kind=core):
        return ((b * 4 + a) * (1 - kind) + (a * 4 + b) * kind) * 2 + kind

    def ring(i):
        return (i + 4) % 4

    sibling = row + 1 - 2 * core
    devices = lead_all.shape[0] // lead.shape[0]
    rows, piece, line = lead.shape[0], far_all.shape[0] // devices, charge.shape[0]

    barrier = pltpu.get_barrier_semaphore()

    def greet(i, carry):
        pl.semaphore_signal(barrier, inc=1, device_id=((row + i) % devices, col), device_id_type=MESH)
        return carry

    lax.fori_loop(1, devices, greet, 0)
    pl.semaphore_wait(barrier, devices - 1)

    def cut(ref, owner, size):
        return ref.at[pl.ds(pl.multiple_of(owner * size, size), size)]

    def spread(other):
        return pltpu.make_async_remote_copy(
            src_ref=cut(panel, other, piece), dst_ref=cut(far_all, other, piece),
            send_sem=spread_sem.at[other], recv_sem=far_recv.at[other],
            device_id=(other, col), device_id_type=MESH)

    mine = [pltpu.make_async_copy(lead, cut(lead_all, row, rows), local_sem.at[0]),
            pltpu.make_async_copy(charge, cut(charge_all, row, line), local_sem.at[1])]

    started = ([], [], [])
    arrays = [(lead, lead_all, rows, send_sem.at[0], recv_sem.at[0]),
              (charge, charge_all, line, send_sem.at[1], recv_sem.at[1]),
              (None, far_all, piece, far_send, far_recv)]
    kinds = ((0, 1), (2,))

    def send(kind, owner, target, own=False):
        for n in kinds[kind]:
            source, ref, size, out, into = arrays[n]
            copy = pltpu.make_async_remote_copy(
                src_ref=source if own and source is not None else cut(ref, owner, size),
                dst_ref=cut(ref, owner, size),
                send_sem=out.at[len(started[n])], recv_sem=into.at[owner],
                device_id=(target, col), device_id_type=MESH)
            copy.start()
            started[n].append(copy)

    def arrived(kind, owner):
        for n in kinds[kind]:
            _, ref, size, _, into = arrays[n]
            pltpu.make_async_copy(cut(ref, owner, size), cut(ref, owner, size), into.at[owner]).wait()

    def across(kind, owner, own=False):
        send(kind, owner, place(u, ring(v + 1)), own)
        send(kind, owner, place(u, ring(v - 1)), own)
        send(kind, owner, sibling, own)

    def own(kind):
        send(kind, row, place(ring(u + 1), v), True)
        send(kind, row, place(ring(u - 1), v), True)
        across(kind, row, True)

    def first(kind):
        e = (1 - 2 * kind) * (2 * (u % 2) - 1)
        owner = place(ring(u - e), v)
        arrived(kind, owner)
        send(kind, owner, place(ring(u + e), v))
        across(kind, owner)
        for a in (ring(u + e), ring(u + 2)):
            owner = place(a, v)
            arrived(kind, owner)
            across(kind, owner)

    def second(kind):
        f = (1 - 2 * kind) * (2 * (v % 2) - 1)
        order = [u, ring(u + 1), ring(u - 1), ring(u + 2)]
        for a in order:
            owner = place(a, ring(v - f))
            arrived(kind, owner)
            send(kind, owner, place(u, ring(v + f)))
            send(kind, owner, sibling)
            owner = place(a, ring(v + f))
            arrived(kind, owner)
            send(kind, owner, sibling)
        for a in order:
            owner = place(a, ring(v + 2))
            arrived(kind, owner)
            send(kind, owner, sibling)

    own(0)
    for copy in mine:
        copy.start()

    @pl.when(row == col)
    def _():
        def go(i, carry):
            spread((row + i) % devices).start()
            return carry

        lax.fori_loop(1, devices, go, 0)
        pltpu.make_async_copy(cut(panel, row, piece), cut(far_all, row, piece), far_recv.at[row]).start()

    first(0)
    arrived(1, row)
    own(1)
    second(0)
    first(1)
    second(1)
    for kind in (0, 1):
        for a in range(4):
            for b in range(4):
                arrived(kind, place(a, b, 1 - core))
    for copy in mine:
        copy.wait()
    for group in started:
        for copy in group:
            copy.wait_send()

    @pl.when(row == col)
    def _():
        def end(i, carry):
            spread((row + i) % devices).wait_send()
            return carry

        lax.fori_loop(1, devices, end, 0)


def gathered(lead_block, panel_block, charge_lead):
    devices = lax.axis_size("row")
    vmem = pl.BlockSpec(memory_space=pltpu.VMEM)
    hbm = pl.BlockSpec(memory_space=pl.ANY)
    tall = lambda a: jax.ShapeDtypeStruct((a.shape[0] * devices, a.shape[1]), F32)
    dma = pltpu.SemaphoreType.DMA
    return pl.pallas_call(
        gather,
        out_shape=[tall(lead_block), jax.ShapeDtypeStruct(panel_block.shape, F32), tall(charge_lead)],
        in_specs=[hbm] * 3,
        out_specs=[vmem] * 3,
        scratch_shapes=[dma((2, devices - 1)), dma((2, devices)), dma((devices - 1,)), dma((devices,)),
                        dma((devices,)), dma((2,))],
        compiler_params=pltpu.CompilerParams(collective_id=0, has_side_effects=True, vmem_limit_bytes=20 * 2**20),
    )(lead_block, panel_block, charge_lead)


def shards(lead_block, panel_block, trailing_slab, charge_lead, charge_rest):
    lead_whole, far, charge_whole = gathered(lead_block, panel_block, charge_lead)
    vmem = pl.BlockSpec(memory_space=pltpu.VMEM)
    hbm = pl.BlockSpec(memory_space=pl.ANY)
    like = lambda a: jax.ShapeDtypeStruct(a.shape, F32)
    lead_mine, lower_panel, slab, solved, rest = pl.pallas_call(
        kernel,
        out_shape=[like(lead_block), like(panel_block), like(trailing_slab), like(charge_lead), like(charge_rest)],
        in_specs=[hbm] * 6,
        out_specs=[vmem, hbm, vmem, vmem, vmem],
        scratch_shapes=[
            pltpu.VMEM(lead_whole.shape, F32),
            pltpu.VMEM((2 * panel_block.shape[0], panel_block.shape[1]), F32),
            pltpu.VMEM(charge_whole.shape, F32),
            pltpu.SemaphoreType.DMA((6,)),
            pltpu.SemaphoreType.DMA,
        ],
        compiler_params=pltpu.CompilerParams(vmem_limit_bytes=56 * 2**20),
    )(lead_whole, panel_block, far, charge_whole, trailing_slab, charge_rest)
    return lead_mine, lower_panel, slab, solved, rest


def solution(mesh):
    placed = (P("row", None), P("row", None), P("row", "col"), P("row", "col"), P("row", "col"))
    return jax.shard_map(shards, mesh=mesh, in_specs=placed, out_specs=placed, check_vma=False)
```

```python
import collections
import jax
import jax.numpy as jnp
from jax import lax
from jax.experimental import pallas as pl
from jax.experimental.pallas import tpu as pltpu
from jax.sharding import PartitionSpec as P

F32, BF16 = jnp.float32, jnp.bfloat16
B = 128
BLOCKS = 8


def lane(x, i):
    return jnp.broadcast_to(x[:, i:i + 1], (8, B))


def sub(x, j):
    return jnp.broadcast_to(x[j:j + 1, :], (8, B))


def factor(rows, upper, inverse):
    row_of = lax.broadcasted_iota(jnp.int32, (8, B), 0)
    lane_of = lax.broadcasted_iota(jnp.int32, (8, B), 1)
    n = len(rows)
    own = [lane(rows[0], i) for i in range(8)]
    for g in range(n):
        here = (lane_of >= 8 * g) & (lane_of < 8 * g + 8)
        unit = jnp.where(lane_of == row_of + 8 * g, 1.0, 0.0)
        a = jnp.where(here, unit, rows[g])
        if g + 1 < n:
            below = [lane(rows[g + 1], 8 * g + i) for i in range(8)]
            after = [lane(rows[g + 1], 8 * g + 8 + i) for i in range(8)]
        dinv = None
        for j in range(8):
            heads = {i: sub(own[i], j) for i in range(j, 8)}
            r = 1.0 / heads[j]
            dinv = r if j == 0 else jnp.where(row_of == j, r, dinv)
            m = jnp.where(row_of > j, own[j] * r, 0.0)
            for i in range(j + 1, 8):
                own[i] = own[i] - m * heads[i]
            if j < 7:
                a = a - m * sub(a, j)
            if g + 1 < n:
                mn = below[j] * r
                for i in range(j + 1, 8):
                    below[i] = below[i] - mn * heads[i]
                for i in range(8):
                    after[i] = after[i] - mn * sub(below[j], i)
            yield
        scale = jnp.sqrt(dinv)
        corner = own[0]
        for i in range(1, 8):
            corner = jnp.where(lane_of == 8 * g + i, own[i], corner)
        corner = jnp.where(lane_of >= row_of + 8 * g, corner, 0.0)
        upper.append(jnp.where(lane_of < 8 * g + 8, jnp.where(here, corner, 0.0), a) * scale)
        inverse.append(jnp.where(lane_of < 8 * g + 8, a, 0.0) * scale)
        if g + 1 < n:
            z = a * dinv
            for j in range(7, 0, -1):
                t = jnp.where(row_of < j, own[j] * dinv, 0.0)
                z = z - t * sub(z, j)
            s = [sub(z, i) for i in range(8)]
            for h in range(g + 1, n):
                p = [lane(rows[h], 8 * g + i) * s[i] for i in range(8)]
                rows[h] = jnp.where(here, 0.0, rows[h]) - (
                    ((p[0] + p[1]) + (p[2] + p[3])) + ((p[4] + p[5]) + (p[6] + p[7])))
            own = after


def two(x):
    h = x.astype(BF16)
    return h, (x - h.astype(F32)).astype(BF16)


def three(x):
    h = x.astype(BF16)
    r = x - h.astype(F32)
    m = r.astype(BF16)
    return h, m, (r - m.astype(F32)).astype(BF16)


def left6(x):
    h, m, l = three(x)
    return jnp.concatenate([h, h, m, h, m, l], 1)


def right6(x, axis=0):
    h, m, l = three(x)
    return jnp.concatenate([h, m, h, l, m, h], axis)


def left4(x):
    h, l = two(x)
    return jnp.concatenate([h, l, h, l], 1)


def right4(x, axis=0):
    h, l = two(x)
    return jnp.concatenate([h, h, l, l], axis)


def parts(count):
    odd = count % 2
    lefts = [(n, p) for n in range(count - odd) for p in (0, 1, 0)]
    rights = [(n, p) for n in range(count - odd) for p in (0, 0, 1)]
    if odd:
        lefts += [(count - 1, p) for p in (0, 1, 0, 1)]
        rights += [(count - 1, p) for p in (0, 0, 1, 1)]
    return lefts, rights


def mul(x, y):
    return jnp.dot(x, y, preferred_element_type=F32)


def mul_t(x, y):
    return lax.dot_general(x, y, (((1,), (1,)), ((), ())), preferred_element_type=F32)


def at(i):
    return slice(i * B, i * B + B)


class Plan:
    def __init__(self, s, z, c, t, r, xs, us, ys, rows, ready, leave):
        self.s, self.z, self.c, self.t, self.r = s, z, c, t, r
        self.xs, self.us, self.ys = xs, us, ys
        self.rows, self.ready, self.leave = rows, ready, leave
        self.queue = collections.deque()

    def drain(self, count=None):
        while self.queue and (count is None or count > 0):
            self.queue.popleft()()
            if count is not None:
                count -= 1

    def step(self, k):
        s = self.s
        rows = [s[k * B + 8 * g:k * B + 8 * g + 8, at(k)] for g in range(16)]
        upper, inverse = [], []
        total = len(self.queue)
        done = 0
        for n, _ in enumerate(factor(rows, upper, inverse)):
            due = min(total, (n + 1) * total // 124)
            self.drain(due - done)
            done = due
        self.drain()
        self.ready(k)
        self.after(k, jnp.concatenate(upper, 0), jnp.concatenate(inverse, 0))

    def rights_of(self, k, first, count, cols):
        _, rights = parts(count)
        return jnp.concatenate([self.us[p, at(first + n), cols] for n, p in rights], 0)

    def lefts_of(self, rows, first, count):
        lefts, _ = parts(count)
        return jnp.concatenate([self.xs[p, rows, at(first + n)] for n, p in lefts], 1)

    def after(self, k, upper, w):
        s, z, c, t, r, half = self.s, self.z, self.c, self.t, self.r, self.rows
        xs, us, ys = self.xs, self.us, self.ys
        add = self.queue.append
        wl = left6(w)
        w4 = right4(w, 1)
        last = BLOCKS - 1
        ql, pr = {}, {}

        def panel(j):
            p = mul(wl, right6(s[at(k), at(j)]))
            h, m, l = three(p)
            pr[j] = jnp.concatenate([h, m, h, l, m, h], 0)
            us[0, at(k), at(j)] = h
            us[1, at(k), at(j)] = m
            q = p.T
            s[at(j), at(k)] = q
            ql[j] = left6(q)

        def trail(i, j):
            s[at(i), at(j)] = s[at(i), at(j)] - mul(ql[i], pr[j])

        def diagonal():
            s[at(k), at(k)] = upper.T

        def solve(m):
            rows = slice(m * 256, m * 256 + 256)
            x = mul_t(left4(z[rows, at(k)]), w4)
            z[rows, at(k)] = x
            h, l = two(x)
            xs[0, rows, at(k)] = h
            xs[1, rows, at(k)] = l

        def build(m):
            rows = slice(m * 256, m * 256 + 256)
            z[rows, at(k + 1)] = z[rows, at(k + 1)] - mul(
                self.lefts_of(rows, 0, k + 1), self.rights_of(k, 0, k + 1, at(k + 1)))

        def right():
            y = mul(left4(w), right4(c[at(k), :]))
            c[at(k), :] = y
            h, l = two(y)
            ys[0, at(k), :] = h
            ys[1, at(k), :] = l

        def right_below(i):
            h, l = ys[0, at(k), :], ys[1, at(k), :]
            c[at(i), :] = c[at(i), :] - mul(left4(s[at(i), at(k)]), jnp.concatenate([h, h, l, l], 0))

        def slab(m, n, first, count):
            rows = slice(m * 256, m * 256 + 256)
            cols = slice(n * 256, n * 256 + 256)
            lefts, rights = parts(count)
            far = slice(half + n * 256, half + n * 256 + 256)
            x = jnp.concatenate([xs[p, far, at(first + i)] for i, p in rights], 1)
            t[rows, cols] = t[rows, cols] - mul_t(self.lefts_of(rows, first, count), x)

        def rest(m, first, count):
            rows = slice(m * 256, m * 256 + 256)
            _, rights = parts(count)
            y = jnp.concatenate([ys[p, at(first + n), :] for n, p in rights], 0)
            r[rows, :] = r[rows, :] - mul(self.lefts_of(rows, first, count), y)

        if k < last:
            panel(k + 1)
            trail(k + 1, k + 1)
            for j in range(k + 2, BLOCKS):
                add(lambda j=j: panel(j))
            for j in range(k + 2, BLOCKS):
                add(lambda j=j: trail(k + 1, j))
        for m in range(2 * half // 256):
            add(lambda m=m: solve(m))
        add(lambda: self.leave(k))
        if k < last:
            for i in range(k + 2, BLOCKS):
                for j in range(i, BLOCKS):
                    add(lambda i=i, j=j: trail(i, j))
        add(right)
        if k < last:
            for m in range(2 * half // 256):
                add(lambda m=m: build(m))
        add(diagonal)
        for i in range(k + 1, BLOCKS):
            add(lambda i=i: right_below(i))
        groups = {1: (0, 2), 3: (2, 2), 5: (4, 2), 6: (6, 1), 7: (7, 1)}
        if k in groups:
            first, count = groups[k]
            for m in range(half // 256):
                for n in range(t.shape[1] // 256):
                    add(lambda m=m, n=n: slab(m, n, first, count))
            for m in range(half // 256):
                add(lambda m=m: rest(m, first, count))


def whole(s, z, c, t, r, xs, us, ys, rows, ready, leave):
    plan = Plan(s, z, c, t, r, xs, us, ys, rows, ready, leave)
    for k in range(BLOCKS):
        plan.step(k)
    plan.drain()


def kernel(lead, panel, far, charge, slab, rest, lead_out, panel_out, slab_out, charge_out, rest_out,
           s, z, c, xs, us, ys, sem, out_sem):
    half = panel.shape[0]
    here = [(lead.at[0:B], s.at[0:B]), (lead.at[B:], s.at[B:]), (panel, z.at[0:half]), (far, z.at[half:2 * half]),
            (charge, c), (slab, slab_out), (rest, rest_out)]
    copies = [pltpu.make_async_copy(a, b, sem.at[i]) for i, (a, b) in enumerate(here)]
    for copy in copies:
        copy.start()
    copies[0].wait()
    leaving = []

    def ready(k):
        if k == 0:
            for copy in copies[1:]:
                copy.wait()

    def leave(k):
        copy = pltpu.make_async_copy(z.at[0:half, at(k)], panel_out.at[:, at(k)], out_sem.at[k])
        copy.start()
        leaving.append(copy)

    whole(s, z, c, slab_out, rest_out, xs, us, ys, half, ready, leave)
    count = lead_out.shape[0]
    first = pl.multiple_of(lax.axis_index("row") * count, count)
    column = lax.broadcasted_iota(jnp.int32, lead_out.shape, 1)
    line = lax.broadcasted_iota(jnp.int32, lead_out.shape, 0) + first
    lead_out[...] = jnp.where(column <= line, s[pl.ds(first, count), :], 0.0)
    charge_out[...] = c[pl.ds(first, count), :]
    for copy in leaving:
        copy.wait()


MESH = pl.DeviceIdType.MESH


def gather(lead, panel, charge, lead_all, far_all, charge_all, send_sem, recv_sem, far_send, far_recv, spread_sem, local_sem):
    row, col = lax.axis_index("row"), lax.axis_index("col")
    planes = lax.axis_size("col")
    core, chip = row % 2, row // 2
    x, y = chip % 4, chip // 4
    u = x * (1 - core) + y * core
    v = y * (1 - core) + x * core

    def place(a, b, kind=core):
        return ((b * 4 + a) * (1 - kind) + (a * 4 + b) * kind) * 2 + kind

    def ring(i):
        return (i + 4) % 4

    sibling = row + 1 - 2 * core
    devices = lead_all.shape[0] // lead.shape[0]
    rows, piece, line = lead.shape[0], far_all.shape[0] // devices, charge.shape[0]

    barrier = pltpu.get_barrier_semaphore()

    share = devices // planes
    source = (col, row // share)
    near = [(place(ring(u + n), v), col) for n in (1, 2, 3)] + [(place(u, ring(v + n)), col) for n in (1, 2, 3)] + [(sibling, col)]
    for other in near:
        pl.semaphore_signal(barrier, inc=1, device_id=other, device_id_type=MESH)
    alone = (row == source[0]) & (col == source[1])

    @pl.when(jnp.logical_not(alone))
    def _():
        pl.semaphore_signal(barrier, inc=1, device_id=source, device_id_type=MESH)

    feeds = row < planes
    peers = jnp.where(feeds, len(near) + share, len(near)) - jnp.where(alone, 1, 0)
    pl.semaphore_wait(barrier, peers)

    def cut(ref, owner, size):
        return ref.at[pl.ds(pl.multiple_of(owner * size, size), size)]

    def spread(other, n):
        return pltpu.make_async_remote_copy(
            src_ref=cut(panel, other, piece), dst_ref=cut(far_all, other, piece),
            send_sem=spread_sem.at[n], recv_sem=far_recv.at[other],
            device_id=(other, row), device_id_type=MESH)

    mine = [pltpu.make_async_copy(lead, cut(lead_all, row, rows), local_sem.at[0]),
            pltpu.make_async_copy(charge, cut(charge_all, row, line), local_sem.at[1])]

    started = ([], [], [])
    arrays = [(lead, lead_all, rows, send_sem.at[0], recv_sem.at[0]),
              (charge, charge_all, line, send_sem.at[1], recv_sem.at[1]),
              (None, far_all, piece, far_send, far_recv)]
    kinds = ((0, 1), (2,))

    def send(kind, owner, target, own=False):
        for n in kinds[kind]:
            source, ref, size, out, into = arrays[n]
            copy = pltpu.make_async_remote_copy(
                src_ref=source if own and source is not None else cut(ref, owner, size),
                dst_ref=cut(ref, owner, size),
                send_sem=out.at[len(started[n])], recv_sem=into.at[owner],
                device_id=(target, col), device_id_type=MESH)
            copy.start()
            started[n].append(copy)

    def arrived(kind, owner):
        for n in kinds[kind]:
            _, ref, size, _, into = arrays[n]
            pltpu.make_async_copy(cut(ref, owner, size), cut(ref, owner, size), into.at[owner]).wait()

    def across(kind, owner, own=False):
        send(kind, owner, place(u, ring(v + 1)), own)
        send(kind, owner, place(u, ring(v - 1)), own)
        send(kind, owner, place(u, ring(v + 2)), own)
        send(kind, owner, sibling, own)

    def own(kind):
        send(kind, row, place(ring(u + 1), v), True)
        send(kind, row, place(ring(u - 1), v), True)
        send(kind, row, place(ring(u + 2), v), True)
        across(kind, row, True)

    def first(kind):
        e = (1 - 2 * kind) * (2 * (u % 2) - 1)
        owner = place(ring(u - e), v)
        arrived(kind, owner)
        across(kind, owner)
        for a in (ring(u + e), ring(u + 2)):
            owner = place(a, v)
            arrived(kind, owner)
            across(kind, owner)

    def second(kind):
        f = (1 - 2 * kind) * (2 * (v % 2) - 1)
        order = [u, ring(u + 1), ring(u - 1), ring(u + 2)]
        for a in order:
            owner = place(a, ring(v - f))
            arrived(kind, owner)
            send(kind, owner, sibling)
            owner = place(a, ring(v + f))
            arrived(kind, owner)
            send(kind, owner, sibling)
        for a in order:
            owner = place(a, ring(v + 2))
            arrived(kind, owner)
            send(kind, owner, sibling)

    own(0)
    for copy in mine:
        copy.start()

    for n in range(devices // lax.axis_size("col")):
        target = col * share + n

        @pl.when(feeds & ((target != row) | (row != col)))
        def _():
            spread(target, n).start()

    @pl.when(alone)
    def _():
        pltpu.make_async_copy(cut(panel, row, piece), cut(far_all, row, piece), far_recv.at[row]).start()

    first(0)
    arrived(1, row)
    own(1)
    second(0)
    first(1)
    second(1)
    for kind in (0, 1):
        for a in range(4):
            for b in range(4):
                arrived(kind, place(a, b, 1 - core))
    for copy in mine:
        copy.wait()
    for group in started:
        for copy in group:
            copy.wait_send()

    for n in range(devices // lax.axis_size("col")):
        target = col * share + n

        @pl.when(feeds & ((target != row) | (row != col)))
        def _():
            spread(target, n).wait_send()


def gathered(lead_block, panel_block, charge_lead):
    devices = lax.axis_size("row")
    vmem = pl.BlockSpec(memory_space=pltpu.VMEM)
    hbm = pl.BlockSpec(memory_space=pl.ANY)
    tall = lambda a: jax.ShapeDtypeStruct((a.shape[0] * devices, a.shape[1]), F32)
    dma = pltpu.SemaphoreType.DMA
    return pl.pallas_call(
        gather,
        out_shape=[tall(lead_block), jax.ShapeDtypeStruct(panel_block.shape, F32), tall(charge_lead)],
        in_specs=[hbm] * 3,
        out_specs=[hbm] * 3,
        scratch_shapes=[dma((2, devices - 1)), dma((2, devices)), dma((devices - 1,)), dma((devices,)),
                        dma((devices,)), dma((2,))],
        compiler_params=pltpu.CompilerParams(collective_id=0, has_side_effects=True, vmem_limit_bytes=60 * 2**20),
    )(lead_block, panel_block, charge_lead)


def shards(lead_block, panel_block, trailing_slab, charge_lead, charge_rest):
    lead_whole, far, charge_whole = gathered(lead_block, panel_block, charge_lead)
    vmem = pl.BlockSpec(memory_space=pltpu.VMEM)
    hbm = pl.BlockSpec(memory_space=pl.ANY)
    like = lambda a: jax.ShapeDtypeStruct(a.shape, F32)
    half, width = panel_block.shape
    return tuple(pl.pallas_call(
        kernel,
        out_shape=[like(lead_block), like(panel_block), like(trailing_slab), like(charge_lead), like(charge_rest)],
        in_specs=[hbm] * 6,
        out_specs=[vmem, hbm, vmem, vmem, vmem],
        scratch_shapes=[
            pltpu.VMEM(lead_whole.shape, F32),
            pltpu.VMEM((2 * half, width), F32),
            pltpu.VMEM(charge_whole.shape, F32),
            pltpu.VMEM((2, 2 * half, width), BF16),
            pltpu.VMEM((2,) + lead_whole.shape, BF16),
            pltpu.VMEM((2,) + charge_whole.shape, BF16),
            pltpu.SemaphoreType.DMA((7,)),
            pltpu.SemaphoreType.DMA((BLOCKS,)),
        ],
        compiler_params=pltpu.CompilerParams(vmem_limit_bytes=60 * 2**20),
    )(lead_whole, panel_block, far, charge_whole, trailing_slab, charge_rest))


def solution(mesh):
    placed = (P("row", None), P("row", None), P("row", "col"), P("row", "col"), P("row", "col"))
    return jax.shard_map(shards, mesh=mesh, in_specs=placed, out_specs=placed, check_vma=False)
```
